256 devices in a mesh: rows: 16 (over x_lo, z), vox: 16 (over x_hi, y, core).
Axes of the slice: x: 4 (x_hi: 2, x_lo: 2; x = x_hi * 2 + x_lo), y: 4, z: 8, core: 2. Of those that a mesh axis runs over, the one named last changes fastest.
Arguments:
- system: float32 [2048, 262144], P('rows', 'vox'), may hold values from -0.01171875 to 0.01171875
- measured: float32 [128, 2048], P(None, 'rows'), may hold values from -18 to 18
- start_image: float32 [128, 262144], P('rows', 'vox'), may hold values from 0 to 1
Outputs:
- image: float32 [128, 262144], P('rows', 'vox')
The draws below stay inside these ranges and needn't reach their ends.
All inputs are finite; a program needn't handle non-finite values.
Results may differ from the reference program's by a relative error of at most 0.0003.
Values sent between devices are 32-bit elements; how exact they have to be, the bound alone decides.
No kernel may reach another device: no remote copies, remote signals or barrier semaphores. Data moves between devices by JAX's collectives and lax.ppermute only.
A program may use at most 64 MiB of HBM per device.

```python
import jax
import jax.numpy as jnp
from jax import lax

ROWS_DEV = 128
FRONT = 8
NV = 262144
M = 2048
F = 128
N_ROWS = 16


def block_scale(own_key, shape, cuts, least, largest):
    factor_of = 1.0
    for position, blocks in cuts:
        draws = jax.random.uniform(jax.random.fold_in(jax.random.fold_in(own_key, 6), position), (blocks,), jnp.float32, least / len(cuts), largest / len(cuts))
        factor_of = factor_of * jnp.repeat(jnp.exp(draws), shape[position] // blocks).reshape((-1,) + (1,) * (len(shape) - 1 - position))
    return factor_of


def gaussian(rng, extent, width, most, shards=(), kind=jnp.bfloat16):
    entries = jax.random.normal(rng, extent, jnp.float32) * width
    if len(shards) > 0:
        entries = block_scale(rng, extent, shards, -0.22, 0.18) * entries
    return jnp.clip(entries, min=-most, max=most).astype(kind)


def setup_inputs(seed: int = 0) -> dict:
    key_of = jax.random.split(jax.random.key(seed), 4)
    system = gaussian(key_of[0], (M, NV), NV ** -0.5, 0.01171875, ((0, 16), (1, 16)), jnp.float32)
    measured = gaussian(key_of[1], (F, M), 3.0, 18.0, ((1, 16),), jnp.float32)
    start_image = jnp.clip(1.0 * jax.random.uniform(key_of[2], (F, NV), jnp.float32) ** block_scale(key_of[2], (F, NV), ((0, 16), (1, 16)), -0.2, 0.2), 0.0, 1.0)
    return {"system": system, "measured": measured, "start_image": start_image}


lower_bound = 0.0
upper_bound = 1.0


def reference(system, measured, start_image):
    def one_front(front_index):
        first = (front_index * FRONT).astype(jnp.int32)
        current = lax.dynamic_slice_in_dim(start_image, first, FRONT, 0)
        signals = lax.dynamic_slice_in_dim(measured, first, FRONT, 0)

        def visit(tick_index, current):
            block_index = ((front_index + tick_index) % N_ROWS).astype(jnp.int32)
            offset = (block_index * ROWS_DEV).astype(jnp.int32)
            matrix_tile = lax.dynamic_slice_in_dim(system, offset, ROWS_DEV, 0)
            wanted = lax.dynamic_slice_in_dim(signals, offset, ROWS_DEV, 1)
            product = lax.dot_general(current, matrix_tile, (((1,), (1,)), ((), ())), precision=lax.Precision.HIGHEST)
            residual = wanted - product
            update = jnp.dot(residual, matrix_tile, precision=lax.Precision.HIGHEST)
            return jnp.clip(current + update, lower_bound, upper_bound)

        return lax.fori_loop(0, N_ROWS, visit, current)

    fronts = lax.map(one_front, jnp.arange(N_ROWS, dtype=jnp.int32))
    return fronts.reshape(N_ROWS * FRONT, fronts.shape[2])
```

```python
import functools

import jax
import jax.numpy as jnp
from jax import lax
from jax.experimental import pallas as pl
from jax.experimental.pallas import tpu as pltpu
from jax.sharding import PartitionSpec as P


lower_bound = 0.0
upper_bound = 1.0

CHUNK = 2048
f32 = jnp.float32
bf16 = jnp.bfloat16
VMEM = pl.BlockSpec(memory_space=pltpu.VMEM)
SMEM = pl.BlockSpec(memory_space=pltpu.SMEM)

HELD = (0, 1, 2, 3, 4, 5, 6, 7, 8, 8, 8, 8, 8, 8, 8, 8)

barrier = lax.optimization_barrier


def gate(value, *others):
    return barrier((value, *others))[0]


def parts_of(value):
    hi = value.astype(bf16)
    return hi, (value - hi.astype(f32)).astype(bf16)


def split_kernel(a_ref, o_ref, *refs):
    sems, copies = refs[-1], refs[:-1]
    moves = [
        pltpu.make_async_copy(a_ref.at[:, pl.ds(c * CHUNK, CHUNK)], copy, sems.at[c])
        for c, copy in enumerate(copies)
    ]
    for move in moves:
        move.start()

    def step(c, _):
        o_ref[c] = jnp.concatenate(parts_of(a_ref[:, at(c)]), axis=0)
        return 0

    lax.fori_loop(0, o_ref.shape[0], step, 0)
    for move in moves:
        move.wait()


def split_rows(system):
    rows, vox = system.shape
    n = vox // CHUNK
    own, *copies = pl.pallas_call(
        split_kernel,
        in_specs=[VMEM],
        out_specs=[VMEM] + [pl.BlockSpec(memory_space=pl.ANY)] * n,
        out_shape=[jax.ShapeDtypeStruct((n, 2 * rows, CHUNK), bf16)]
        + [jax.ShapeDtypeStruct((rows, CHUNK), f32)] * n,
        scratch_shapes=[pltpu.SemaphoreType.DMA((n,))],
        compiler_params=pltpu.CompilerParams(vmem_limit_bytes=8 << 20),
        name="split_rows",
    )(system)
    return own, copies


def arrange_kernel(front_ref, meas_ref, o_ref):
    for k in range(o_ref.shape[0]):
        f = front_ref[k]
        o_ref[k] = meas_ref[pl.ds(pl.multiple_of(f * 8, 8), 8), :]


def arranged(measured, fronts):
    n = fronts.shape[0]
    return pl.pallas_call(
        arrange_kernel,
        in_specs=[SMEM, VMEM],
        out_specs=VMEM,
        out_shape=jax.ShapeDtypeStruct((n, measured.shape[0] // n, measured.shape[1]), f32),
        name="arranged",
    )(fronts, measured)


def turn_kernel(a_ref, *refs):
    o_ref = refs[-1]
    hi, lo = parts_of(a_ref[...])
    o_ref[0] = jnp.concatenate([hi.astype(f32).T.astype(bf16), lo.astype(f32).T.astype(bf16)], axis=1)


def split_turned(index, chunk, store):
    rows = chunk.shape[0]
    shape = (8, CHUNK, 2 * rows) if store is None else store.shape
    operands = [chunk] if store is None else [chunk, store]
    return pl.pallas_call(
        turn_kernel,
        grid=(1,),
        in_specs=[
            pl.BlockSpec(chunk.shape, lambda i: (0, 0)),
            pl.BlockSpec(memory_space=pl.ANY),
        ][: len(operands)],
        out_specs=pl.BlockSpec((1, *shape[1:]), lambda i: (index, 0, 0)),
        out_shape=jax.ShapeDtypeStruct(shape, bf16),
        input_output_aliases={} if store is None else {1: 0},
        compiler_params=pltpu.CompilerParams(vmem_limit_bytes=8 << 20),
        cost_estimate=pl.CostEstimate(flops=1 << 20, bytes_accessed=2 << 20, transcendentals=0),
        name="split_turned",
    )(*operands)


def at(c):
    return pl.ds(pl.multiple_of(c * CHUNK, CHUNK), CHUNK)


def product_kernel(first, turned, add, *refs):
    x_ref, a_ref = refs[0], refs[1]
    o_ref, acc = refs[-2], refs[-1]
    acc[...] = jnp.zeros_like(acc)

    def step(c, _):
        lhs = jnp.concatenate(parts_of(x_ref[:, at(c)]), axis=0)
        if turned:
            acc[...] += jnp.dot(lhs, a_ref[c + first], preferred_element_type=f32)
        else:
            acc[...] += lax.dot_general(
                lhs, a_ref[c + first], (((1,), (1,)), ((), ())), preferred_element_type=f32
            )
        return 0

    lax.fori_loop(0, x_ref.shape[1] // CHUNK, step, 0)
    both = acc[0:8, :] + acc[8:16, :]
    p = both[:, :128] + both[:, 128:]
    o_ref[...] = p + refs[2][...] if add else p


def product(x, a, first, turned, before):
    operands = [x, a] + ([] if before is None else [before])
    return pl.pallas_call(
        functools.partial(product_kernel, first, turned, before is not None),
        in_specs=[VMEM] * len(operands),
        out_specs=VMEM,
        out_shape=jax.ShapeDtypeStruct((8, 128), f32),
        scratch_shapes=[pltpu.VMEM((16, 256), f32)],
        compiler_params=pltpu.CompilerParams(vmem_limit_bytes=4 << 20),
        cost_estimate=pl.CostEstimate(flops=1 << 28, bytes_accessed=4 << 20, transcendentals=0),
        name="product",
    )(*operands)


def update_kernel(k, ins, outs, total_ref, wanted_ref, a_ref, *refs):
    one = jnp.concatenate(parts_of(wanted_ref[k] - total_ref[...]), axis=0)
    lhs = jnp.concatenate([one, one], axis=1)
    cuts = sorted({0, *ins, *outs})

    def piece(sizes, c):
        begin = 0
        for i, end in enumerate(sizes):
            if c < end:
                return i, begin
            begin = end

    for low, high in zip(cuts[:-1], cuts[1:]):
        i, i0 = piece(ins, low)
        o, o0 = piece(outs, low)
        x_ref, o_ref = refs[i], refs[len(ins) + o]

        def step(c, _):
            d = jnp.dot(lhs, a_ref[c], preferred_element_type=f32)
            x = x_ref[:, at(c - i0)] + (d[0:8] + d[8:16])
            o_ref[:, at(c - o0)] = jnp.clip(x, lower_bound, upper_bound)
            return 0

        lax.fori_loop(low, high, step, 0)


def update(k, total, wanted, a, pieces, ins, outs):
    sizes = [e - b for b, e in zip((0, *outs[:-1]), outs)]
    return pl.pallas_call(
        functools.partial(update_kernel, k, ins, outs),
        in_specs=[VMEM] * (3 + len(pieces)),
        out_specs=[VMEM] * len(outs),
        out_shape=[jax.ShapeDtypeStruct((8, n * CHUNK), f32) for n in sizes],
        compiler_params=pltpu.CompilerParams(vmem_limit_bytes=4 << 20),
        cost_estimate=pl.CostEstimate(flops=1 << 28, bytes_accessed=4 << 20, transcendentals=0),
        name="update",
    )(total, wanted, a, *pieces)


def shifted(block, distance):
    n = lax.axis_size("rows")
    return lax.ppermute(block, "rows", [(i, (i + distance) % n) for i in range(n)])


def exchanged(p, reach):
    n = lax.axis_size("vox")
    return p + lax.ppermute(p, "vox", [(i, i ^ reach) for i in range(n)])


def ends(held, n):
    return tuple(e for e in (held, n) if e > 0) if held < n else (n,)


def shards(system, measured, start_image):
    cycle = lax.axis_size("rows")
    position = lax.axis_index("rows")
    n = system.shape[1] // CHUNK
    fronts = ((position - jnp.arange(cycle)) % cycle).astype(jnp.int32)
    wanted = arranged(measured, fronts)
    own, chunks = split_rows(system)
    arriving = []
    following = None
    pieces, ins, held = [start_image], (n,), 0
    p = product(start_image, own, 0, False, None)
    for k in range(cycle):
        last = k == cycle - 1
        now = 0 if last else HELD[k]
        outs = ends(now, n)
        p = exchanged(p, 8)
        if len(arriving) < n and not last:
            p, chunk = barrier((p, chunks[len(arriving)]))
            arriving.append(shifted(chunk, -1))
        p = exchanged(p, 1)
        for reach in (2, 4):
            p = exchanged(p, reach)
        new = update(k, p, wanted, own, pieces, ins, outs)
        if last:
            return shifted(new[0], 1)
        if now < n:
            far = shifted(new[-1], 1)
        for c in range(held, now):
            following = split_turned(c, gate(arriving[c], p), following)
        held = now
        if now == 0:
            pieces = [far]
            p = product(far, own, 0, False, None)
        else:
            p = product(new[0], following, 0, True, None)
            p, kept = barrier((p, new[0]))
            p = shifted(p, 1)
            near = shifted(kept, 1)
            if now < n:
                p = product(far, own, now, False, p)
                pieces = [near, far]
            else:
                pieces = [near]
        ins = outs


def solution(mesh):
    placed = (P("rows", "vox"), P(None, "rows"), P("rows", "vox"))
    return jax.shard_map(
        shards, mesh=mesh, in_specs=placed, out_specs=P("rows", "vox"), check_vma=False
    )
```

```python
import functools

import jax
import jax.numpy as jnp
from jax import lax
from jax.experimental import pallas as pl
from jax.experimental.pallas import tpu as pltpu
from jax.sharding import PartitionSpec as P


lower_bound = 0.0
upper_bound = 1.0

CHUNK = 2048
f32 = jnp.float32
bf16 = jnp.bfloat16
VMEM = pl.BlockSpec(memory_space=pltpu.VMEM)
SMEM = pl.BlockSpec(memory_space=pltpu.SMEM)

HELD = (0, 1, 2, 3, 4, 5, 6, 7, 8, 8, 8, 8, 8, 8, 8, 8)

barrier = lax.optimization_barrier


def gate(value, *others):
    return barrier((value, *others))[0]


def parts_of(value):
    hi = value.astype(bf16)
    return hi, (value - hi.astype(f32)).astype(bf16)


def split_kernel(a_ref, o_ref, *refs):
    sems, copies = refs[-1], refs[:-1]
    moves = [
        pltpu.make_async_copy(a_ref.at[:, pl.ds(c * CHUNK, CHUNK)], copy, sems.at[c])
        for c, copy in enumerate(copies)
    ]
    for move in moves:
        move.start()

    def step(c, _):
        o_ref[c] = jnp.concatenate(parts_of(a_ref[:, at(c)]), axis=0)
        return 0

    lax.fori_loop(0, o_ref.shape[0], step, 0)
    for move in moves:
        move.wait()


def split_rows(system):
    rows, vox = system.shape
    n = vox // CHUNK
    own, *copies = pl.pallas_call(
        split_kernel,
        in_specs=[VMEM],
        out_specs=[VMEM] + [pl.BlockSpec(memory_space=pl.ANY)] * n,
        out_shape=[jax.ShapeDtypeStruct((n, 2 * rows, CHUNK), bf16)]
        + [jax.ShapeDtypeStruct((rows, CHUNK), f32)] * n,
        scratch_shapes=[pltpu.SemaphoreType.DMA((n,))],
        compiler_params=pltpu.CompilerParams(vmem_limit_bytes=8 << 20),
        name="split_rows",
    )(system)
    return own, copies


def arrange_kernel(meas_ref, o_ref):
    n = o_ref.shape[0]
    position = lax.axis_index("rows")
    for k in range(n):
        f = lax.rem(position + (n - k), n)
        o_ref[k] = meas_ref[pl.ds(pl.multiple_of(f * 8, 8), 8), :]


def arranged(measured, n):
    return pl.pallas_call(
        arrange_kernel,
        in_specs=[VMEM],
        out_specs=VMEM,
        out_shape=jax.ShapeDtypeStruct((n, measured.shape[0] // n, measured.shape[1]), f32),
        compiler_params=pltpu.CompilerParams(vmem_limit_bytes=1 << 20),
        name="arranged",
    )(measured)


def turn_kernel(a_ref, *refs):
    o_ref = refs[-1]
    hi, lo = parts_of(a_ref[...])
    o_ref[0] = jnp.concatenate([hi.astype(f32).T.astype(bf16), lo.astype(f32).T.astype(bf16)], axis=1)


def split_turned(index, chunk, store):
    rows = chunk.shape[0]
    shape = (8, CHUNK, 2 * rows) if store is None else store.shape
    operands = [chunk] if store is None else [chunk, store]
    return pl.pallas_call(
        turn_kernel,
        grid=(1,),
        in_specs=[
            pl.BlockSpec(chunk.shape, lambda i: (0, 0)),
            pl.BlockSpec(memory_space=pl.ANY),
        ][: len(operands)],
        out_specs=pl.BlockSpec((1, *shape[1:]), lambda i: (index, 0, 0)),
        out_shape=jax.ShapeDtypeStruct(shape, bf16),
        input_output_aliases={} if store is None else {1: 0},
        compiler_params=pltpu.CompilerParams(vmem_limit_bytes=8 << 20),
        cost_estimate=pl.CostEstimate(flops=1 << 20, bytes_accessed=2 << 20, transcendentals=0),
        name="split_turned",
    )(*operands)


def at(c):
    return pl.ds(pl.multiple_of(c * CHUNK, CHUNK), CHUNK)


def looped(low, high, step):
    lax.fori_loop(low, high, step, 0, unroll=2 if (high - low) % 2 == 0 else 1)


def product_kernel(first, turned, add, *refs):
    x_ref, a_ref = refs[0], refs[1]
    o_ref, acc = refs[-2], refs[-1]
    acc[...] = jnp.zeros_like(acc)

    def step(c, _):
        lhs = jnp.concatenate(parts_of(x_ref[:, at(c)]), axis=0)
        if turned:
            acc[...] += jnp.dot(lhs, a_ref[c + first], preferred_element_type=f32)
        else:
            acc[...] += lax.dot_general(
                lhs, a_ref[c + first], (((1,), (1,)), ((), ())), preferred_element_type=f32
            )
        return 0

    looped(0, x_ref.shape[1] // CHUNK, step)
    both = acc[0:8, :] + acc[8:16, :]
    p = both[:, :128] + both[:, 128:]
    o_ref[...] = p + refs[2][...] if add else p


def product(x, a, first, turned, before):
    operands = [x, a] + ([] if before is None else [before])
    return pl.pallas_call(
        functools.partial(product_kernel, first, turned, before is not None),
        in_specs=[VMEM] * len(operands),
        out_specs=VMEM,
        out_shape=jax.ShapeDtypeStruct((8, 128), f32),
        scratch_shapes=[pltpu.VMEM((16, 256), f32)],
        compiler_params=pltpu.CompilerParams(vmem_limit_bytes=4 << 20),
        cost_estimate=pl.CostEstimate(flops=1 << 28, bytes_accessed=4 << 20, transcendentals=0),
        name="product",
    )(*operands)


def update_kernel(k, ins, outs, total_ref, wanted_ref, a_ref, *refs):
    one = jnp.concatenate(parts_of(wanted_ref[k] - total_ref[...]), axis=0)
    lhs = jnp.concatenate([one, one], axis=1)
    cuts = sorted({0, *ins, *outs})

    def piece(sizes, c):
        begin = 0
        for i, end in enumerate(sizes):
            if c < end:
                return i, begin
            begin = end

    for low, high in zip(cuts[:-1], cuts[1:]):
        i, i0 = piece(ins, low)
        o, o0 = piece(outs, low)
        x_ref, o_ref = refs[i], refs[len(ins) + o]

        def step(c, _):
            d = jnp.dot(lhs, a_ref[c], preferred_element_type=f32)
            x = x_ref[:, at(c - i0)] + (d[0:8] + d[8:16])
            o_ref[:, at(c - o0)] = jnp.clip(x, lower_bound, upper_bound)
            return 0

        looped(low, high, step)


def update(k, total, wanted, a, pieces, ins, outs):
    sizes = [e - b for b, e in zip((0, *outs[:-1]), outs)]
    return pl.pallas_call(
        functools.partial(update_kernel, k, ins, outs),
        in_specs=[VMEM] * (3 + len(pieces)),
        out_specs=[VMEM] * len(outs),
        out_shape=[jax.ShapeDtypeStruct((8, n * CHUNK), f32) for n in sizes],
        compiler_params=pltpu.CompilerParams(vmem_limit_bytes=4 << 20),
        cost_estimate=pl.CostEstimate(flops=1 << 28, bytes_accessed=4 << 20, transcendentals=0),
        name="update",
    )(total, wanted, a, *pieces)


def shifted(block, distance):
    n = lax.axis_size("rows")
    return lax.ppermute(block, "rows", [(i, (i + distance) % n) for i in range(n)])


def shifted_across(block, reach):
    n, m = lax.axis_size("rows"), lax.axis_size("vox")
    pairs = [(r * m + v, (r + 1) % n * m + (v ^ reach)) for r in range(n) for v in range(m)]
    return lax.ppermute(block, ("rows", "vox"), pairs)


def exchanged(p, reach):
    n = lax.axis_size("vox")
    return p + lax.ppermute(p, "vox", [(i, i ^ reach) for i in range(n)])


def ends(held, n):
    return tuple(e for e in (held, n) if e > 0) if held < n else (n,)


def shards(system, measured, start_image):
    cycle = lax.axis_size("rows")
    n = system.shape[1] // CHUNK
    wanted = arranged(measured, cycle)
    own, chunks = split_rows(system)
    arriving = []
    following = None
    pieces, ins, held, crossed = [start_image], (n,), 0, False
    p = product(start_image, own, 0, False, None)
    for k in range(cycle):
        last = k == cycle - 1
        now = 0 if last else HELD[k]
        outs = ends(now, n)
        if not crossed:
            p = exchanged(p, 8)
        if len(arriving) < n and not last:
            p, chunk = barrier((p, chunks[len(arriving)]))
            arriving.append(shifted(chunk, -1))
        p = exchanged(p, 1)
        for reach in (2, 4):
            p = exchanged(p, reach)
        new = update(k, p, wanted, own, pieces, ins, outs)
        if last:
            return shifted(new[0], 1)
        if now < n:
            far = shifted(new[-1], 1)
        for c in range(held, now):
            following = split_turned(c, gate(arriving[c], p), following)
        held = now
        if now == 0:
            pieces = [far]
            p = product(far, own, 0, False, None)
        else:
            p = product(new[0], following, 0, True, None)
            p, kept = barrier((p, new[0]))
            crossed = now == n
            if crossed:
                across = shifted_across(p, 8)
            p = shifted(p, 1)
            if crossed:
                p = p + across
            near = shifted(kept, 1)
            if now < n:
                p = product(far, own, now, False, p)
                pieces = [near, far]
            else:
                pieces = [near]
        ins = outs


def solution(mesh):
    placed = (P("rows", "vox"), P(None, "rows"), P("rows", "vox"))
    return jax.shard_map(
        shards, mesh=mesh, in_specs=placed, out_specs=P("rows", "vox"), check_vma=False
    )
```

```python
import functools

import jax
import jax.numpy as jnp
from jax import lax
from jax.experimental import pallas as pl
from jax.experimental.pallas import tpu as pltpu
from jax.sharding import PartitionSpec as P


lower_bound = 0.0
upper_bound = 1.0

CHUNK = 2048
f32 = jnp.float32
bf16 = jnp.bfloat16
VMEM = pl.BlockSpec(memory_space=pltpu.VMEM)
SMEM = pl.BlockSpec(memory_space=pltpu.SMEM)

HELD = (0, 1, 2, 3, 4, 5, 6, 7, 8, 8, 8, 8, 8, 8, 8, 8)

barrier = lax.optimization_barrier


def gate(value, *others):
    return barrier((value, *others))[0]


def parts_of(value):
    hi = value.astype(bf16)
    return hi, (value - hi.astype(f32)).astype(bf16)


def split_kernel(a_ref, o_ref, *refs):
    sems, copies = refs[-1], refs[:-1]
    moves = [
        pltpu.make_async_copy(a_ref.at[:, pl.ds(c * CHUNK, CHUNK)], copy, sems.at[c])
        for c, copy in enumerate(copies)
    ]
    for move in moves:
        move.start()

    def step(c, _):
        o_ref[c] = jnp.concatenate(parts_of(a_ref[:, at(c)]), axis=0)
        return 0

    lax.fori_loop(0, o_ref.shape[0], step, 0)
    for move in moves:
        move.wait()


def split_rows(system):
    rows, vox = system.shape
    n = vox // CHUNK
    own, *copies = pl.pallas_call(
        split_kernel,
        in_specs=[VMEM],
        out_specs=[VMEM] + [pl.BlockSpec(memory_space=pl.ANY)] * n,
        out_shape=[jax.ShapeDtypeStruct((n, 2 * rows, CHUNK), bf16)]
        + [jax.ShapeDtypeStruct((rows, CHUNK), f32)] * n,
        scratch_shapes=[pltpu.SemaphoreType.DMA((n,))],
        compiler_params=pltpu.CompilerParams(vmem_limit_bytes=8 << 20),
        name="split_rows",
    )(system)
    return own, copies


def arrange_kernel(meas_ref, o_ref):
    n = o_ref.shape[0]
    position = lax.axis_index("rows")
    for k in range(n):
        f = lax.rem(position + (n - k), n)
        o_ref[k] = meas_ref[pl.ds(pl.multiple_of(f * 8, 8), 8), :]


def arranged(measured, n):
    return pl.pallas_call(
        arrange_kernel,
        in_specs=[VMEM],
        out_specs=VMEM,
        out_shape=jax.ShapeDtypeStruct((n, measured.shape[0] // n, measured.shape[1]), f32),
        compiler_params=pltpu.CompilerParams(vmem_limit_bytes=1 << 20),
        name="arranged",
    )(measured)


def turn_kernel(a_ref, *refs):
    o_ref = refs[-1]
    hi, lo = parts_of(a_ref[...])
    o_ref[0] = jnp.concatenate([hi.astype(f32).T.astype(bf16), lo.astype(f32).T.astype(bf16)], axis=1)


def split_turned(index, chunk, store):
    rows = chunk.shape[0]
    shape = (8, CHUNK, 2 * rows) if store is None else store.shape
    operands = [chunk] if store is None else [chunk, store]
    return pl.pallas_call(
        turn_kernel,
        grid=(1,),
        in_specs=[
            pl.BlockSpec(chunk.shape, lambda i: (0, 0)),
            pl.BlockSpec(memory_space=pl.ANY),
        ][: len(operands)],
        out_specs=pl.BlockSpec((1, *shape[1:]), lambda i: (index, 0, 0)),
        out_shape=jax.ShapeDtypeStruct(shape, bf16),
        input_output_aliases={} if store is None else {1: 0},
        compiler_params=pltpu.CompilerParams(vmem_limit_bytes=8 << 20),
        cost_estimate=pl.CostEstimate(flops=1 << 20, bytes_accessed=2 << 20, transcendentals=0),
        name="split_turned",
    )(*operands)


def at(c):
    return pl.ds(pl.multiple_of(c * CHUNK, CHUNK), CHUNK)


def looped(low, high, step):
    lax.fori_loop(low, high, step, 0, unroll=2 if (high - low) % 2 == 0 else 1)


def product_kernel(first, turned, pieces, add, *refs):
    a_ref = refs[pieces]
    o_ref, acc = refs[-2], refs[-1]
    acc[...] = jnp.zeros_like(acc)
    begin = first
    for x_ref in refs[:pieces]:

        def step(c, _, x_ref=x_ref, begin=begin):
            lhs = jnp.concatenate(parts_of(x_ref[:, at(c)]), axis=0)
            if turned:
                acc[...] += jnp.dot(lhs, a_ref[c + begin], preferred_element_type=f32)
            else:
                acc[...] += lax.dot_general(
                    lhs, a_ref[c + begin], (((1,), (1,)), ((), ())), preferred_element_type=f32
                )
            return 0

        count = x_ref.shape[1] // CHUNK
        looped(0, count, step)
        begin += count
    both = acc[0:8, :] + acc[8:16, :]
    p = both[:, :128] + both[:, 128:]
    o_ref[...] = p + refs[pieces + 1][...] if add else p


def product(xs, a, first, turned, before):
    operands = [*xs, a] + ([] if before is None else [before])
    return pl.pallas_call(
        functools.partial(product_kernel, first, turned, len(xs), before is not None),
        in_specs=[VMEM] * len(operands),
        out_specs=VMEM,
        out_shape=jax.ShapeDtypeStruct((8, 128), f32),
        scratch_shapes=[pltpu.VMEM((16, 256), f32)],
        compiler_params=pltpu.CompilerParams(vmem_limit_bytes=4 << 20),
        cost_estimate=pl.CostEstimate(flops=1 << 28, bytes_accessed=4 << 20, transcendentals=0),
        name="product",
    )(*operands)


def update_kernel(k, ins, outs, total_ref, wanted_ref, a_ref, *refs):
    one = jnp.concatenate(parts_of(wanted_ref[k] - total_ref[...]), axis=0)
    lhs = jnp.concatenate([one, one], axis=1)
    cuts = sorted({0, *ins, *outs})

    def piece(sizes, c):
        begin = 0
        for i, end in enumerate(sizes):
            if c < end:
                return i, begin
            begin = end

    for low, high in zip(cuts[:-1], cuts[1:]):
        i, i0 = piece(ins, low)
        o, o0 = piece(outs, low)
        x_ref, o_ref = refs[i], refs[len(ins) + o]

        def step(c, _):
            d = jnp.dot(lhs, a_ref[c], preferred_element_type=f32)
            x = x_ref[:, at(c - i0)] + (d[0:8] + d[8:16])
            o_ref[:, at(c - o0)] = jnp.clip(x, lower_bound, upper_bound)
            return 0

        looped(low, high, step)


def update(k, total, wanted, a, pieces, ins, outs):
    sizes = [e - b for b, e in zip((0, *outs[:-1]), outs)]
    return pl.pallas_call(
        functools.partial(update_kernel, k, ins, outs),
        in_specs=[VMEM] * (3 + len(pieces)),
        out_specs=[VMEM] * len(outs),
        out_shape=[jax.ShapeDtypeStruct((8, n * CHUNK), f32) for n in sizes],
        compiler_params=pltpu.CompilerParams(vmem_limit_bytes=4 << 20),
        cost_estimate=pl.CostEstimate(flops=1 << 28, bytes_accessed=4 << 20, transcendentals=0),
        name="update",
    )(total, wanted, a, *pieces)


def shifted(block, distance):
    n = lax.axis_size("rows")
    return lax.ppermute(block, "rows", [(i, (i + distance) % n) for i in range(n)])


def shifted_across(block, reach):
    n, m = lax.axis_size("rows"), lax.axis_size("vox")
    pairs = [(r * m + v, (r + 1) % n * m + (v ^ reach)) for r in range(n) for v in range(m)]
    return lax.ppermute(block, ("rows", "vox"), pairs)


def from_partner(p, reach):
    n = lax.axis_size("vox")
    return lax.ppermute(p, "vox", [(i, i ^ reach) for i in range(n)])


def summed_four(p):
    c = from_partner(p, 4)
    b = from_partner(p, 2)
    d = from_partner(p, 6)
    return (p + b) + (c + d)


def ends(held, n, last):
    if last or held == n:
        return (2, 4, n), 3
    far = n - held
    cuts = (held + far // 2, n) if far > 3 else (n,)
    return ((held, *cuts), 1) if held else (cuts, 0)


def shards(system, measured, start_image):
    cycle = lax.axis_size("rows")
    n = system.shape[1] // CHUNK
    wanted = arranged(measured, cycle)
    own, chunks = split_rows(system)
    arriving = []
    following = None
    pieces, ins, held, crossed = [start_image], (n,), 0, False
    p = product(pieces, own, 0, False, None)
    for k in range(cycle):
        last = k == cycle - 1
        now = 0 if last else HELD[k]
        outs, count = ends(now, n, last)
        if not crossed:
            p = p + from_partner(p, 8)
        if len(arriving) < n and not last:
            p, chunk = barrier((p, chunks[len(arriving)]))
            arriving.append(shifted(chunk, -1))
        p = p + from_partner(p, 1)
        p = summed_four(p)
        new = update(k, p, wanted, own, pieces, ins, outs)
        ins = outs
        if last:
            return jnp.concatenate([shifted(x, 1) for x in new], axis=1)
        if now < n:
            far = [shifted(x, 1) for x in new[count:]]
        for c in range(held, now):
            following = split_turned(c, gate(arriving[c], p), following)
        held = now
        if now == 0:
            pieces = far
            p = product(far, own, 0, False, None)
            continue
        crossed = now == n
        if crossed:
            first = [shifted(new[0], 1)]
            rest = new[1:]
            p = product(new, following, 0, True, None)
        else:
            first, rest = [], new[:count]
            p = product(rest, following, 0, True, None)
        p, *rest = barrier((p, *rest))
        if crossed:
            across = shifted_across(p, 8)
        p = shifted(p, 1)
        near = first + [shifted(x, 1) for x in rest]
        if crossed:
            p = p + across
            pieces = near
        else:
            p = product(far, own, now, False, p)
            pieces = near + far


def solution(mesh):
    placed = (P("rows", "vox"), P(None, "rows"), P("rows", "vox"))
    return jax.shard_map(
        shards, mesh=mesh, in_specs=placed, out_specs=P("rows", "vox"), check_vma=False
    )
```
